32 devices in a mesh: rep: 2 (over x), blk: 16 (over z, y, core).
Axes of the slice: x: 2, y: 2, z: 4, core: 2. Of those that a mesh axis runs over, the one named last changes fastest.
Arguments:
- features: bfloat16 [4096, 512], P(('rep', 'blk')), may hold values from -6 to 6
- weight: bfloat16 [512, 512], replicated, may hold values from -0.25 to 0.25
- tile_values: bfloat16 [2, 16, 16, 2, 128, 128], P('rep', 'blk'), as said below
- tile_list: int32 [2, 16, 16, 2], P('rep', 'blk'), may hold values from -1 to 1, as said below
- train_mask: int32 [4096], P(('rep', 'blk')), may hold values 0 or 1
- cotangent: bfloat16 [4096, 512], P(('rep', 'blk')), may hold values from -6 to 6
Outputs:
- activated: bfloat16 [4096, 512], P(('rep', 'blk'))
- weight_grad: float32 [512, 512], replicated
- feature_grad: bfloat16 [4096, 512], P(('rep', 'blk'))
The draws below stay inside these ranges and needn't reach their ends.
Inputs may be any that keep to these rules, and one draw needn't show every extreme that they name: `tile_list`: -1 marks an empty slot; 0 or 1 names the half h whose tile [r, b, j, h] is nonempty; the two slots of a pair never name the same half. The graph is undirected: block (u, v) of A is nonempty exactly when block (v, u) is, and every block (u, u) is nonempty. How many nonempty tiles a device holds differs from device to device. `tile_values`: the tile of block (u, v) is the transpose of the tile of block (v, u), so A is symmetric.
All inputs are finite; a program needn't handle non-finite values. No bound on the sum of `train_mask` on one device may be relied on, other than what follows from the above.
Results may differ from the reference program's by a relative error of at most 0.014.
Values may be sent and summed in bfloat16 or wider, within the bound.
A program may use at most 128 MiB of HBM per device.

```python
import math
import jax
import jax.numpy as jnp
from jax import lax

F = 512
TILE = 128
NODES = 4096
N_REP = 2
N_BLK = 16


def draw_tile_values(key, part):
    device_count = N_REP * N_BLK
    base = jax.random.normal(key, (device_count, device_count, TILE, TILE), jnp.float32)
    flipped = jnp.transpose(base, (1, 0, 3, 2))
    row_ids = jnp.arange(device_count)[:, None, None, None]
    col_ids = jnp.arange(device_count)[None, :, None, None]
    symmetric = jnp.where(row_ids < col_ids, base, jnp.where(row_ids > col_ids, flipped, (base + flipped) * 0.70710678))
    scaled = symmetric * (1.0 / math.sqrt(TILE * N_BLK))
    shaped = scaled.reshape(N_REP, N_BLK, N_REP, N_BLK, TILE, TILE)
    return jnp.transpose(shaped, (2, 1, 3, 0, 4, 5)).astype(jnp.bfloat16)


def draw_tile_list(key, part):
    device_count = N_REP * N_BLK
    base = jax.random.randint(jax.random.fold_in(key, 11), (device_count, device_count), 0, 8)
    row_ids = jnp.arange(device_count)[:, None]
    col_ids = jnp.arange(device_count)[None, :]
    symmetric = jnp.where(row_ids < col_ids, base, base.T)
    levels = jax.random.randint(jax.random.fold_in(key, 12), (device_count,), 0, 4)
    linked = (symmetric + levels[:, None] + levels[None, :] >= 7) | (row_ids == col_ids)
    shaped = jnp.transpose(linked.reshape(N_REP, N_BLK, N_REP, N_BLK), (2, 1, 3, 0))
    first_slot = jnp.where(shaped[..., 0], 0, -1)
    second_slot = jnp.where(shaped[..., 1], 1, -1)
    swapped = jax.random.randint(jax.random.fold_in(key, 13), (N_REP, N_BLK, N_BLK), 0, 2)
    slot_zero = jnp.where(swapped == 1, second_slot, first_slot)
    slot_one = jnp.where(swapped == 1, first_slot, second_slot)
    return jnp.stack([slot_zero, slot_one], axis=-1).astype(jnp.int32)


def set_ends(values, own_key, least, top_value):
    place = [jax.random.randint(jax.random.fold_in(own_key, axis), (), 0, length) for axis, length in enumerate(values.shape)]
    widest = values.shape.index(max(values.shape))
    neighbour = place[:widest] + [(place[widest] + 1) % values.shape[widest]] + place[widest + 1:]
    return values.at[tuple(place)].set(least).at[tuple(neighbour)].set(top_value)


def block_levels(key, dims, pieces, smallest, high):
    factor_of, own = 1.0, jax.random.fold_in(key, 6)
    for axis_at, parts in pieces:
        steps = jnp.exp(jax.random.uniform(jax.random.fold_in(own, axis_at), (parts,), jnp.float32, smallest / len(pieces), high / len(pieces)))
        factor_of = factor_of * jnp.repeat(steps, dims[axis_at] // parts).reshape([-1 if axis == axis_at else 1 for axis in range(len(dims))])
    return factor_of


def bell_draw(stream_key, extent, spread, limit, cuts=(), kind=jnp.bfloat16):
    factor_of = block_levels(stream_key, extent, cuts, -0.22, 0.18) if cuts else 1.0
    result = jax.random.normal(stream_key, extent, jnp.float32) * spread * factor_of
    return jnp.minimum(jnp.maximum(result, -limit), limit).astype(kind)


def setup_inputs(seed: int = 0) -> dict:
    arg_keys = jax.random.split(jax.random.key(seed), 7)
    features = bell_draw(arg_keys[0], (NODES, F), 1.0, 6.0, ((0, 32),))
    weight = bell_draw(arg_keys[1], (F, F), F ** -0.5, 0.25)
    tile_values = draw_tile_values(jax.random.fold_in(arg_keys[6], 71), 0)
    tile_list = draw_tile_list(jax.random.fold_in(arg_keys[6], 71), 0)
    train_mask = set_ends((jax.random.randint(arg_keys[4], (NODES,), 0, 2) < 1).astype(jnp.int32), jax.random.fold_in(arg_keys[4], 1), 0, 1)
    cotangent = bell_draw(arg_keys[5], (NODES, F), 1.0, 6.0, ((0, 32),))
    return dict(features=features, weight=weight, tile_values=tile_values, tile_list=tile_list, train_mask=train_mask, cotangent=cotangent)


GELU_SCALE = math.sqrt(2.0 / math.pi)

def activation(pre_act):
    inner = GELU_SCALE * (pre_act + 0.044715 * pre_act * pre_act * pre_act)
    tanh_part = jnp.tanh(inner)
    act_value = 0.5 * pre_act * (1.0 + tanh_part)
    act_slope = 0.5 * (1.0 + tanh_part) + 0.5 * pre_act * (1.0 - tanh_part * tanh_part) * GELU_SCALE * (1.0 + 3.0 * 0.044715 * pre_act * pre_act)
    return (act_value, act_slope)

def reference(features, weight, tile_values, tile_list, train_mask, cotangent):
    half_zero = jnp.any(tile_list == 0, axis=-1)
    half_one = jnp.any(tile_list == 1, axis=-1)
    presence = jnp.stack([half_zero, half_one], axis=-1).astype(tile_values.dtype)
    masked = tile_values * presence[..., None, None]
    projected = jnp.dot(features, weight, preferred_element_type=jnp.float32).astype(jnp.bfloat16)
    proj_blocks = projected.reshape(N_REP, N_BLK, TILE, F).astype(jnp.float32)

    def one_group(block_id):
        tiles_here = lax.dynamic_index_in_dim(masked, block_id, 1, keepdims=False).astype(jnp.float32)
        return jnp.einsum('rjhst,rjtf->hsf', tiles_here, proj_blocks)
    grouped = lax.map(one_group, jnp.arange(N_BLK, dtype=jnp.int32))
    summed = jnp.transpose(grouped, (1, 0, 2, 3)).reshape(NODES, F)
    act_value, act_slope = activation(summed)
    activated = act_value.astype(jnp.bfloat16)
    grad_z = (cotangent.astype(jnp.float32) * train_mask.astype(jnp.float32)[:, None] * act_slope).astype(jnp.bfloat16)
    grad_blocks = grad_z.reshape(N_REP, N_BLK, TILE, F).astype(jnp.float32)

    def one_column(column_id):
        tiles_here = lax.dynamic_index_in_dim(masked, column_id, 2, keepdims=False).astype(jnp.float32)
        return jnp.einsum('rbhst,hbsf->rtf', tiles_here, grad_blocks)
    columns = lax.map(one_column, jnp.arange(N_BLK, dtype=jnp.int32))
    prop_grad = jnp.transpose(columns, (1, 0, 2, 3)).reshape(NODES, F).astype(jnp.bfloat16)
    weight_grad = jnp.dot(features.T, prop_grad, preferred_element_type=jnp.float32)
    feature_grad = jnp.dot(prop_grad, weight.T, preferred_element_type=jnp.float32).astype(jnp.bfloat16)
    return (activated, weight_grad, feature_grad)
```

```python
import functools
import math

import jax
import jax.numpy as jnp
from jax import lax
from jax.experimental import pallas as pl
from jax.experimental.pallas import tpu as pltpu
from jax.sharding import PartitionSpec as P

GELU_SCALE = math.sqrt(2.0 / math.pi)
CHUNKS = 2
MESH = pl.DeviceIdType.MESH


def activation(pre_act):
    inner = GELU_SCALE * (pre_act + 0.044715 * pre_act * pre_act * pre_act)
    tanh_part = jnp.tanh(inner)
    act_value = 0.5 * pre_act * (1.0 + tanh_part)
    act_slope = 0.5 * (1.0 + tanh_part) + 0.5 * pre_act * (
        1.0 - tanh_part * tanh_part
    ) * GELU_SCALE * (1.0 + 3.0 * 0.044715 * pre_act * pre_act)
    return (act_value, act_slope)


def kernel(
    n_blk, chunks,
    list_ref, mask_ref, x_ref, w_ref, tiles_ref, cot_ref,
    act_ref, wgrad_ref, fgrad_ref,
    xg, gg, wg, w_vm, tiles_vm, cot_vm, a2d, part, axs, axr, qs, qr,
    t_send, t_recv, wxs, wxr, ax_b, act_vm,
    local_sem, x_send, x_recv, g_send, g_recv, w_send, w_recv, wz_send,
    t_ssem, t_rsem, e_send, e_recv,
):
    nz = n_blk // 4
    rows = x_ref.shape[0]
    feat = x_ref.shape[1]
    fc = feat // chunks
    sl = feat // n_blk
    r = lax.axis_index("rep")
    me = lax.axis_index("blk")
    z = me // 4
    y = (me // 2) % 2
    core = me % 2

    def at(zz, yy, cc):
        return zz * 4 + yy * 2 + cc

    y_dev = at(z, 1 - y, core)
    p_dev = at(z, y, 1 - core)

    loads = [
        pltpu.make_async_copy(
            x_ref.at[:, pl.ds(c * fc, fc)], xg.at[c, me], local_sem.at[c]
        )
        for c in range(chunks)
    ]
    others = [
        pltpu.make_async_copy(tiles_ref, tiles_vm, local_sem.at[chunks]),
        pltpu.make_async_copy(w_ref, w_vm, local_sem.at[chunks + 1]),
        pltpu.make_async_copy(cot_ref, cot_vm, local_sem.at[chunks + 2]),
    ]
    for copy in loads + others:
        copy.start()

    barrier = pltpu.get_barrier_semaphore()
    for k in range(1, n_blk):
        pl.semaphore_signal(
            barrier, inc=1, device_id=(r, (me + k) % n_blk), device_id_type=MESH
        )
    pl.semaphore_signal(barrier, inc=1, device_id=(1 - r, me), device_id_type=MESH)
    for copy in loads:
        copy.wait()
    pl.semaphore_wait(barrier, n_blk)

    pending = []

    def send(cond, make):
        if cond is None:
            make().start()
        else:
            @pl.when(cond)
            def _():
                make().start()
        pending.append((cond, make))

    def block_copy(buf, ssem, rsem, slot, c, way, dev):
        def make():
            return pltpu.make_async_remote_copy(
                src_ref=buf(c, slot), dst_ref=buf(c, slot),
                send_sem=ssem.at[c, slot, way], recv_sem=rsem.at[c, slot],
                device_id=(r, dev), device_id_type=MESH,
            )
        return make

    def wait_block(buf, ssem, rsem, slot, c):
        pltpu.make_async_remote_copy(
            src_ref=buf(c, slot), dst_ref=buf(c, slot),
            send_sem=ssem.at[c, slot, 0], recv_sem=rsem.at[c, slot],
            device_id=(r, y_dev), device_id_type=MESH,
        ).wait_recv()

    def gather_own(buf, ssem, rsem, c):
        send(z < nz - 1, block_copy(buf, ssem, rsem, me, c, 0, at(z + 1, y, core)))
        send(z > 0, block_copy(buf, ssem, rsem, me, c, 1, at(z - 1, y, core)))
        send(None, block_copy(buf, ssem, rsem, me, c, 2, y_dev))
        send(None, block_copy(buf, ssem, rsem, me, c, 3, p_dev))

    def from_y(buf, ssem, rsem, zz, c, cond):
        slot = at(zz, 1 - y, core)
        go = block_copy(buf, ssem, rsem, slot, c, 3, p_dev)
        if cond is None:
            wait_block(buf, ssem, rsem, slot, c)
            go().start()
        else:
            @pl.when(cond)
            def _():
                wait_block(buf, ssem, rsem, slot, c)
                go().start()
        pending.append((cond, go))

    def from_z(buf, ssem, rsem, d, c, up):
        zz = z - d if up else z + d
        cond = (zz >= 0) if up else (zz < nz)
        slot = at(zz, y, core)
        nxt = z + 1 if up else z - 1
        more = (nxt < nz) if up else (nxt >= 0)
        go_z = block_copy(buf, ssem, rsem, slot, c, 0 if up else 1, at(nxt, y, core))
        go_y = block_copy(buf, ssem, rsem, slot, c, 2, y_dev)
        go_p = block_copy(buf, ssem, rsem, slot, c, 3, p_dev)

        @pl.when(cond)
        def _():
            wait_block(buf, ssem, rsem, slot, c)

            @pl.when(more)
            def _():
                go_z().start()

            go_y().start()
            go_p().start()

        pending.append((jnp.logical_and(cond, more), go_z))
        pending.append((cond, go_y))
        pending.append((cond, go_p))

    def gather_rest(buf, ssem, rsem):
        for d in range(1, nz):
            for c in range(chunks):
                from_z(buf, ssem, rsem, d, c, True)
                from_z(buf, ssem, rsem, d, c, False)
                if d == 1:
                    from_y(buf, ssem, rsem, z, c, None)
                else:
                    from_y(buf, ssem, rsem, z - d + 1, c, z - d + 1 >= 0)
                    from_y(buf, ssem, rsem, z + d - 1, c, z + d - 1 < nz)

    def gather_last(buf, ssem, rsem, c):
        d = nz
        if d == 1:
            from_y(buf, ssem, rsem, z, c, None)
        else:
            from_y(buf, ssem, rsem, z - d + 1, c, z - d + 1 >= 0)
            from_y(buf, ssem, rsem, z + d - 1, c, z + d - 1 < nz)
        for yy in range(2):
            for zz in range(nz):
                wait_block(buf, ssem, rsem, at(zz, yy, 1 - core), c)

    def exchange(src, dst, k):
        def make():
            return pltpu.make_async_remote_copy(
                src_ref=src, dst_ref=dst, send_sem=e_send.at[k], recv_sem=e_recv.at[k],
                device_id=(1 - r, me), device_id_type=MESH,
            )
        return make

    def xbuf(c, slot):
        return xg.at[c, slot]

    def gbuf(c, slot):
        return gg.at[c, slot]

    def wbuf(c, slot):
        return wg.at[slot, :, pl.ds(c * fc, fc)]

    for c in range(chunks):
        gather_own(xbuf, x_send, x_recv, c)

    others[0].wait()
    for j in range(n_blk):
        for h in range(2):
            here = jnp.logical_or(list_ref[2 * j] == h, list_ref[2 * j + 1] == h)
            keep = jnp.where(here, 1.0, 0.0).astype(jnp.float32)
            tile = tiles_vm[j, h * rows:(h + 1) * rows, :].astype(jnp.float32) * keep
            a2d[h * rows:(h + 1) * rows, j * rows:(j + 1) * rows] = tile.astype(jnp.bfloat16)

    gather_rest(xbuf, x_send, x_recv)
    ax_sends = []
    for c in range(chunks):
        gather_last(xbuf, x_send, x_recv, c)
        total = jnp.dot(
            a2d[:2 * rows, :], xg[c].reshape(n_blk * rows, fc),
            preferred_element_type=jnp.float32,
        )
        part[c] = total.reshape(2, rows, fc)
        axs[c] = part[c, 1 - r].astype(jnp.bfloat16)
        make = exchange(axs.at[c], axr.at[c], c)
        send(None, make)
        ax_sends.append(make)

    others[1].wait()
    others[2].wait()
    mask_cols = jnp.transpose(
        jnp.broadcast_to(mask_ref[...].astype(jnp.float32), (rows, rows))
    )
    for c in range(chunks):
        ax_sends[c]().wait_recv()
        ax = part[c, r] + axr[c].astype(jnp.float32)
        ax_b[:, c * fc:(c + 1) * fc] = ax.astype(jnp.bfloat16)
        slices = jnp.transpose(ax).reshape(fc // sl, sl, rows)
        t_send[c * (fc // sl):(c + 1) * (fc // sl)] = slices.astype(jnp.bfloat16)

    for c in range(chunks):
        summed = jnp.dot(
            ax_b[...], w_vm[:, c * fc:(c + 1) * fc], preferred_element_type=jnp.float32
        )
        act_value, act_slope = activation(summed)
        act_ref[:, c * fc:(c + 1) * fc] = act_value.astype(jnp.bfloat16)
        keep = jnp.concatenate([mask_cols] * (fc // rows), axis=1)
        cot = cot_vm[:, c * fc:(c + 1) * fc].astype(jnp.float32)
        gg[c, me] = (cot * keep * act_slope).astype(jnp.bfloat16)
        gather_own(gbuf, g_send, g_recv, c)

    t_copies = []
    for k in range(1, n_blk):
        peer = (me + k) % n_blk
        def t_make(peer=peer, k=k):
            return pltpu.make_async_remote_copy(
                src_ref=t_send.at[peer], dst_ref=t_recv.at[me],
                send_sem=t_ssem.at[k], recv_sem=t_rsem.at[k],
                device_id=(r, peer), device_id_type=MESH,
            )
        send(None, t_make)
        t_copies.append(t_make)
    t_recv[me] = t_send[me]

    gather_rest(gbuf, g_send, g_recv)
    for k in range(1, n_blk):
        origin = (me + n_blk - k) % n_blk
        pltpu.make_async_remote_copy(
            src_ref=t_send.at[origin], dst_ref=t_recv.at[origin],
            send_sem=t_ssem.at[k], recv_sem=t_rsem.at[k],
            device_id=(r, origin), device_id_type=MESH,
        ).wait_recv()
    for j in range(n_blk):
        a2d[2 * rows:2 * rows + sl, j * rows:(j + 1) * rows] = t_recv[j]

    q_makes, w_makes = [], []
    for c in range(chunks):
        gather_last(gbuf, g_send, g_recv, c)
        total = jnp.dot(
            a2d[...], gg[c].reshape(n_blk * rows, fc), preferred_element_type=jnp.float32
        )
        wxs[c] = total[2 * rows:, :].astype(jnp.bfloat16)
        make = exchange(wxs.at[c], wxr.at[c], chunks + c)
        send(None, make)
        w_makes.append(make)
        part[c] = total[:2 * rows, :].reshape(2, rows, fc)
        qs[c] = part[c, 1 - r].astype(jnp.bfloat16)
        make = exchange(qs.at[c], qr.at[c], 2 * chunks + c)
        send(None, make)
        q_makes.append(make)

    for c in range(chunks):
        w_makes[c]().wait_recv()
        both = wxs[c].astype(jnp.float32) + wxr[c].astype(jnp.float32)
        wg[me, :, c * fc:(c + 1) * fc] = both.astype(jnp.bfloat16)
        for zz in range(nz):
            def z_make(zz=zz, c=c):
                return pltpu.make_async_remote_copy(
                    src_ref=wbuf(c, me), dst_ref=wbuf(c, me),
                    send_sem=wz_send.at[c, zz], recv_sem=w_recv.at[c, me],
                    device_id=(r, at(zz, y, core)), device_id_type=MESH,
                )
            send(z != zz, z_make)
        send(None, block_copy(wbuf, w_send, w_recv, me, c, 0, y_dev))
        send(None, block_copy(wbuf, w_send, w_recv, me, c, 1, p_dev))

    fgrad = jnp.zeros((rows, feat), jnp.float32)
    for c in range(chunks):
        q_makes[c]().wait_recv()
        prop = (part[c, r] + qr[c].astype(jnp.float32)).astype(jnp.bfloat16)
        fgrad = fgrad + lax.dot_general(
            prop, w_vm[:, c * fc:(c + 1) * fc], (((1,), (1,)), ((), ())),
            preferred_element_type=jnp.float32,
        )
    fgrad_ref[...] = fgrad.astype(jnp.bfloat16)

    for c in range(chunks):
        for d in range(1, nz):
            for up in (True, False):
                zz = z - d if up else z + d
                cond = (zz >= 0) if up else (zz < nz)
                slot = at(zz, y, core)
                go_y = block_copy(wbuf, w_send, w_recv, slot, c, 0, y_dev)
                go_p = block_copy(wbuf, w_send, w_recv, slot, c, 1, p_dev)

                @pl.when(cond)
                def _():
                    wait_block(wbuf, w_send, w_recv, slot, c)
                    go_y().start()
                    go_p().start()

                pending.append((cond, go_y))
                pending.append((cond, go_p))
        for zz in range(nz):
            slot = at(zz, 1 - y, core)
            go_p = block_copy(wbuf, w_send, w_recv, slot, c, 1, p_dev)
            wait_block(wbuf, w_send, w_recv, slot, c)
            go_p().start()
            pending.append((None, go_p))
    for c in range(chunks):
        for yy in range(2):
            for zz in range(nz):
                wait_block(wbuf, w_send, w_recv, at(zz, yy, 1 - core), c)
    wgrad_ref[...] = wg[...]

    for cond, make in pending:
        if cond is None:
            make().wait_send()
        else:
            @pl.when(cond)
            def _():
                make().wait_send()


def on_device(features, weight, tile_values, tile_list, train_mask, cotangent, n_blk):
    rows, feat = features.shape
    chunks = CHUNKS
    fc = feat // chunks
    sl = feat // n_blk
    bf = jnp.bfloat16
    vm = pltpu.VMEM
    dma = pltpu.SemaphoreType.DMA
    any_spec = pl.BlockSpec(memory_space=pl.ANY)
    vmem_spec = pl.BlockSpec(memory_space=pltpu.VMEM)
    act, wgrad, fgrad = pl.pallas_call(
        functools.partial(kernel, n_blk, chunks),
        out_shape=(
            jax.ShapeDtypeStruct((rows, feat), bf),
            jax.ShapeDtypeStruct((n_blk, sl, feat), bf),
            jax.ShapeDtypeStruct((rows, feat), bf),
        ),
        in_specs=[
            pl.BlockSpec(memory_space=pltpu.SMEM), vmem_spec,
            any_spec, any_spec, any_spec, any_spec,
        ],
        out_specs=(vmem_spec, vmem_spec, vmem_spec),
        scratch_shapes=[
            vm((chunks, n_blk, rows, fc), bf),
            vm((chunks, n_blk, rows, fc), bf),
            vm((n_blk, sl, feat), bf),
            vm((feat, feat), bf),
            vm((n_blk, 2 * rows, rows), bf),
            vm((rows, feat), bf),
            vm((2 * rows + sl, n_blk * rows), bf),
            vm((chunks, 2, rows, fc), jnp.float32),
            vm((chunks, rows, fc), bf),
            vm((chunks, rows, fc), bf),
            vm((chunks, rows, fc), bf),
            vm((chunks, rows, fc), bf),
            vm((n_blk, sl, rows), bf),
            vm((n_blk, sl, rows), bf),
            vm((chunks, sl, fc), bf),
            vm((chunks, sl, fc), bf),
            vm((rows, feat), bf),
            vm((8, 128), bf),
            dma((chunks + 3,)),
            dma((chunks, n_blk, 4)), dma((chunks, n_blk)),
            dma((chunks, n_blk, 4)), dma((chunks, n_blk)),
            dma((chunks, n_blk, 2)), dma((chunks, n_blk)),
            dma((chunks, n_blk // 4)),
            dma((n_blk,)), dma((n_blk,)),
            dma((3 * chunks,)), dma((3 * chunks,)),
        ],
        compiler_params=pltpu.CompilerParams(
            collective_id=0, has_side_effects=True, vmem_limit_bytes=56 * 1024 * 1024
        ),
    )(
        tile_list.reshape(-1), train_mask.reshape(1, rows), features, weight,
        tile_values.reshape(n_blk, 2 * rows, rows), cotangent,
    )
    return act, wgrad.reshape(feat, feat).astype(jnp.float32), fgrad


def solution(mesh):
    in_specs = (
        P(("rep", "blk"), None),
        P(),
        P("rep", "blk", None, None, None, None),
        P("rep", "blk", None, None),
        P(("rep", "blk")),
        P(("rep", "blk"), None),
    )
    out_specs = (P(("rep", "blk"), None), P(), P(("rep", "blk"), None))
    body = functools.partial(on_device, n_blk=mesh.shape["blk"])
    return jax.shard_map(
        body, mesh=mesh, in_specs=in_specs, out_specs=out_specs, check_vma=False
    )
```

```python
import functools
import math

import jax
import jax.numpy as jnp
from jax import lax
from jax.experimental import pallas as pl
from jax.experimental.pallas import tpu as pltpu
from jax.sharding import PartitionSpec as P

GELU_SCALE = math.sqrt(2.0 / math.pi)
CHUNKS = 2
X_CHUNKS = 2
G_CHUNKS = 2
W_CHUNKS = 1
T_EARLY = 0
NEAR = 1
FIN = 1
MESH = pl.DeviceIdType.MESH


def activation(pre_act):
    inner = GELU_SCALE * (pre_act + 0.044715 * pre_act * pre_act * pre_act)
    tanh_part = jnp.tanh(inner)
    act_value = 0.5 * pre_act * (1.0 + tanh_part)
    act_slope = 0.5 * (1.0 + tanh_part) + 0.5 * pre_act * (
        1.0 - tanh_part * tanh_part
    ) * GELU_SCALE * (1.0 + 3.0 * 0.044715 * pre_act * pre_act)
    return (act_value, act_slope)


def kernel(
    n_blk, chunks, xc, gc, wc,
    list_ref, mask_ref, x_ref, w_ref, tiles_ref, cot_ref,
    act_ref, wgrad_ref, fgrad_ref,
    xg, gg, wg, w_vm, tiles_vm, cot_vm, a2d, part, axs, axr, qs, qr,
    t_send, t_recv, wxs, wxr, ax_b, act_vm,
    local_sem, x_send, x_recv, g_send, g_recv, w_send, w_recv, wz_send,
    t_ssem, t_rsem, e_send, e_recv,
):
    nz = n_blk // 4
    rows = x_ref.shape[0]
    feat = x_ref.shape[1]
    fc = feat // chunks
    sl = feat // n_blk
    r = lax.axis_index("rep")
    me = lax.axis_index("blk")
    z = me // 4
    y = (me // 2) % 2
    core = me % 2

    def at(zz, yy, cc):
        return zz * 4 + yy * 2 + cc

    y_dev = at(z, 1 - y, core)
    p_dev = at(z, y, 1 - core)

    loads = [
        pltpu.make_async_copy(x_ref, xg.at[me], local_sem.at[3])
    ]
    others = [
        pltpu.make_async_copy(tiles_ref, tiles_vm, local_sem.at[0]),
        pltpu.make_async_copy(w_ref, w_vm, local_sem.at[1]),
        pltpu.make_async_copy(cot_ref, cot_vm, local_sem.at[2]),
    ]
    for copy in loads + others:
        copy.start()

    barrier = pltpu.get_barrier_semaphore()
    if NEAR:
        near = [(None, y_dev), (None, p_dev), (z > 0, at(z - 1, y, core)),
                (z < nz - 1, at(z + 1, y, core))]
    else:
        near = [(None, (me + k) % n_blk) for k in range(1, n_blk)]
    for cond, dev in near:
        def greet(dev=dev):
            pl.semaphore_signal(barrier, inc=1, device_id=(r, dev), device_id_type=MESH)
        if cond is None:
            greet()
        else:
            pl.when(cond)(greet)
    pl.semaphore_signal(barrier, inc=1, device_id=(1 - r, me), device_id_type=MESH)
    for copy in loads:
        copy.wait()
    if NEAR:
        ends = (z == 0).astype(jnp.int32) + (z == nz - 1).astype(jnp.int32)
        pl.semaphore_wait(barrier, 5 - ends)
    else:
        pl.semaphore_wait(barrier, n_blk)

    pending = []

    def send(cond, make):
        if cond is None:
            make().start()
        else:
            @pl.when(cond)
            def _():
                make().start()
        pending.append((cond, make))

    def block_copy(buf, ssem, rsem, slot, c, way, dev):
        def make():
            return pltpu.make_async_remote_copy(
                src_ref=buf(c, slot), dst_ref=buf(c, slot),
                send_sem=ssem.at[c, slot, way], recv_sem=rsem.at[c, slot],
                device_id=(r, dev), device_id_type=MESH,
            )
        return make

    def wait_block(buf, ssem, rsem, slot, c):
        pltpu.make_async_remote_copy(
            src_ref=buf(c, slot), dst_ref=buf(c, slot),
            send_sem=ssem.at[c, slot, 0], recv_sem=rsem.at[c, slot],
            device_id=(r, y_dev), device_id_type=MESH,
        ).wait_recv()

    def gather_own(buf, ssem, rsem, c):
        send(z < nz - 1, block_copy(buf, ssem, rsem, me, c, 0, at(z + 1, y, core)))
        send(z > 0, block_copy(buf, ssem, rsem, me, c, 1, at(z - 1, y, core)))
        send(None, block_copy(buf, ssem, rsem, me, c, 2, y_dev))
        send(None, block_copy(buf, ssem, rsem, me, c, 3, p_dev))

    def from_y(buf, ssem, rsem, zz, c, cond):
        slot = at(zz, 1 - y, core)
        go = block_copy(buf, ssem, rsem, slot, c, 3, p_dev)
        if cond is None:
            wait_block(buf, ssem, rsem, slot, c)
            go().start()
        else:
            @pl.when(cond)
            def _():
                wait_block(buf, ssem, rsem, slot, c)
                go().start()
        pending.append((cond, go))

    def from_z(buf, ssem, rsem, d, c, up):
        zz = z - d if up else z + d
        cond = (zz >= 0) if up else (zz < nz)
        slot = at(zz, y, core)
        nxt = z + 1 if up else z - 1
        more = (nxt < nz) if up else (nxt >= 0)
        go_z = block_copy(buf, ssem, rsem, slot, c, 0 if up else 1, at(nxt, y, core))
        go_y = block_copy(buf, ssem, rsem, slot, c, 2, y_dev)
        go_p = block_copy(buf, ssem, rsem, slot, c, 3, p_dev)

        @pl.when(cond)
        def _():
            wait_block(buf, ssem, rsem, slot, c)

            @pl.when(more)
            def _():
                go_z().start()

            go_y().start()
            go_p().start()

        pending.append((jnp.logical_and(cond, more), go_z))
        pending.append((cond, go_y))
        pending.append((cond, go_p))

    def gather_rest(buf, ssem, rsem, chunks):
        for d in range(1, nz):
            for c in range(chunks):
                from_z(buf, ssem, rsem, d, c, True)
                from_z(buf, ssem, rsem, d, c, False)
                if d == 1:
                    from_y(buf, ssem, rsem, z, c, None)
                else:
                    from_y(buf, ssem, rsem, z - d + 1, c, z - d + 1 >= 0)
                    from_y(buf, ssem, rsem, z + d - 1, c, z + d - 1 < nz)

    def gather_last(buf, ssem, rsem, c):
        d = nz
        if d == 1:
            from_y(buf, ssem, rsem, z, c, None)
        else:
            from_y(buf, ssem, rsem, z - d + 1, c, z - d + 1 >= 0)
            from_y(buf, ssem, rsem, z + d - 1, c, z + d - 1 < nz)
        for yy in range(2):
            for zz in range(nz):
                wait_block(buf, ssem, rsem, at(zz, yy, 1 - core), c)

    def exchange(src, dst, k):
        def make():
            return pltpu.make_async_remote_copy(
                src_ref=src, dst_ref=dst, send_sem=e_send.at[k], recv_sem=e_recv.at[k],
                device_id=(1 - r, me), device_id_type=MESH,
            )
        return make

    def xbuf(c, slot):
        return xg.at[slot, :, pl.ds(c * (feat // xc), feat // xc)]

    def gbuf(c, slot):
        return gg.at[slot, :, pl.ds(c * (feat // gc), feat // gc)]

    def wbuf(c, slot):
        return wg.at[slot, :, pl.ds(c * (feat // wc), feat // wc)]

    for c in range(xc):
        gather_own(xbuf, x_send, x_recv, c)

    others[0].wait()
    for j in range(n_blk):
        for h in range(2):
            here = jnp.logical_or(list_ref[0, j] == h, list_ref[1, j] == h)
            keep = jnp.where(here, 1.0, 0.0).astype(jnp.float32)
            tile = tiles_vm[j, h * rows:(h + 1) * rows, :].astype(jnp.float32) * keep
            a2d[h * rows:(h + 1) * rows, j * rows:(j + 1) * rows] = tile.astype(jnp.bfloat16)

    gather_rest(xbuf, x_send, x_recv, xc)
    ax_sends = []
    for c in range(chunks):
        if c < xc:
            gather_last(xbuf, x_send, x_recv, c)
        total = jnp.dot(
            a2d[:2 * rows, :], xg[:, :, c * fc:(c + 1) * fc].reshape(n_blk * rows, fc),
            preferred_element_type=jnp.float32,
        )
        part[c] = total.reshape(2, rows, fc)
        axs[c] = part[c, 1 - r].astype(jnp.bfloat16)
        make = exchange(axs.at[c], axr.at[c], c)
        send(None, make)
        ax_sends.append(make)

    others[1].wait()
    others[2].wait()
    mask_cols = jnp.transpose(
        jnp.broadcast_to(mask_ref[...].astype(jnp.float32), (rows, rows))
    )
    for c in range(chunks):
        ax_sends[c]().wait_recv()
        ax = part[c, r] + axr[c].astype(jnp.float32)
        ax_b[:, c * fc:(c + 1) * fc] = ax.astype(jnp.bfloat16)
        slices = jnp.transpose(ax).reshape(fc // sl, sl, rows)
        t_send[c * (fc // sl):(c + 1) * (fc // sl)] = slices.astype(jnp.bfloat16)

    def send_slices():
        t_copies = []
        for k in range(1, n_blk):
            peer = (me + k) % n_blk
            def t_make(peer=peer, k=k):
                return pltpu.make_async_remote_copy(
                    src_ref=t_send.at[peer], dst_ref=t_recv.at[me],
                    send_sem=t_ssem.at[k], recv_sem=t_rsem.at[k],
                    device_id=(r, peer), device_id_type=MESH,
                )
            send(None, t_make)
            t_copies.append(t_make)
        t_recv[me] = t_send[me]

    if T_EARLY:
        send_slices()

    for c in range(chunks):
        summed = jnp.dot(
            ax_b[...], w_vm[:, c * fc:(c + 1) * fc], preferred_element_type=jnp.float32
        )
        act_value, act_slope = activation(summed)
        act_ref[:, c * fc:(c + 1) * fc] = act_value.astype(jnp.bfloat16)
        keep = jnp.concatenate([mask_cols] * (fc // rows), axis=1)
        cot = cot_vm[:, c * fc:(c + 1) * fc].astype(jnp.float32)
        gg[me, :, c * fc:(c + 1) * fc] = (cot * keep * act_slope).astype(jnp.bfloat16)
        if gc == chunks:
            gather_own(gbuf, g_send, g_recv, c)
    if gc == 1:
        gather_own(gbuf, g_send, g_recv, 0)

    if not T_EARLY:
        send_slices()

    gather_rest(gbuf, g_send, g_recv, gc)
    for k in range(1, n_blk):
        origin = (me + n_blk - k) % n_blk
        pltpu.make_async_remote_copy(
            src_ref=t_send.at[origin], dst_ref=t_recv.at[origin],
            send_sem=t_ssem.at[k], recv_sem=t_rsem.at[k],
            device_id=(r, origin), device_id_type=MESH,
        ).wait_recv()
    for j in range(n_blk):
        a2d[2 * rows:2 * rows + sl, j * rows:(j + 1) * rows] = t_recv[j]

    q_makes, w_makes = [], []
    for c in range(chunks):
        if c < gc:
            gather_last(gbuf, g_send, g_recv, c)
        total = jnp.dot(
            a2d[...], gg[:, :, c * fc:(c + 1) * fc].reshape(n_blk * rows, fc), preferred_element_type=jnp.float32
        )
        wxs[:, c * fc:(c + 1) * fc] = total[2 * rows:, :].astype(jnp.bfloat16)
        if wc == chunks:
            cols = pl.ds(c * fc, fc)
            make = exchange(wxs.at[:, cols], wxr.at[:, cols], chunks + c)
            send(None, make)
            w_makes.append(make)
        elif c == chunks - 1:
            make = exchange(wxs, wxr, chunks)
            send(None, make)
            w_makes.append(make)
        part[c] = total[:2 * rows, :].reshape(2, rows, fc)
        qs[c] = part[c, 1 - r].astype(jnp.bfloat16)
        make = exchange(qs.at[c], qr.at[c], 2 * chunks + c)
        send(None, make)
        q_makes.append(make)

    wf = feat // wc
    for c in range(wc):
        w_makes[c]().wait_recv()
        cols = slice(c * wf, (c + 1) * wf)
        both = wxs[:, cols].astype(jnp.float32) + wxr[:, cols].astype(jnp.float32)
        wg[me, :, cols] = both.astype(jnp.bfloat16)
        for zz in range(nz):
            def z_make(zz=zz, c=c):
                return pltpu.make_async_remote_copy(
                    src_ref=wbuf(c, me), dst_ref=wbuf(c, me),
                    send_sem=wz_send.at[c, zz], recv_sem=w_recv.at[c, me],
                    device_id=(r, at(zz, y, core)), device_id_type=MESH,
                )
            send(z != zz, z_make)
        send(None, block_copy(wbuf, w_send, w_recv, me, c, 0, y_dev))
        send(None, block_copy(wbuf, w_send, w_recv, me, c, 1, p_dev))

    fgrad = jnp.zeros((rows, feat), jnp.float32)
    for c in range(chunks):
        q_makes[c]().wait_recv()
        prop = (part[c, r] + qr[c].astype(jnp.float32)).astype(jnp.bfloat16)
        fgrad = fgrad + lax.dot_general(
            prop, w_vm[:, c * fc:(c + 1) * fc], (((1,), (1,)), ((), ())),
            preferred_element_type=jnp.float32,
        )
    fgrad_ref[...] = fgrad.astype(jnp.bfloat16)

    for c in range(wc):
        for d in range(1, nz):
            for up in (True, False):
                zz = z - d if up else z + d
                cond = (zz >= 0) if up else (zz < nz)
                slot = at(zz, y, core)
                go_y = block_copy(wbuf, w_send, w_recv, slot, c, 0, y_dev)
                go_p = block_copy(wbuf, w_send, w_recv, slot, c, 1, p_dev)

                @pl.when(cond)
                def _():
                    wait_block(wbuf, w_send, w_recv, slot, c)
                    go_y().start()
                    go_p().start()

                pending.append((cond, go_y))
                pending.append((cond, go_p))
        for zz in range(nz):
            slot = at(zz, 1 - y, core)
            go_p = block_copy(wbuf, w_send, w_recv, slot, c, 1, p_dev)
            wait_block(wbuf, w_send, w_recv, slot, c)
            go_p().start()
            pending.append((None, go_p))
    for c in range(wc):
        for yy in range(2):
            for zz in range(nz):
                wait_block(wbuf, w_send, w_recv, at(zz, yy, 1 - core), c)
    wgrad_ref[...] = wg[...]

    for cond, make in pending:
        if cond is None:
            make().wait_send()
        else:
            @pl.when(cond)
            def _():
                make().wait_send()


def widen(act_in, w_in, f_in, act_out, w_out, f_out, act_vm, w_vm, f_vm, wide_vm, in_sem, out_sem):
    ins = [
        pltpu.make_async_copy(src, dst, in_sem.at[i])
        for i, (src, dst) in enumerate(((w_in, w_vm), (act_in, act_vm), (f_in, f_vm)))
    ]
    outs = [
        pltpu.make_async_copy(src, dst, out_sem.at[i])
        for i, (src, dst) in enumerate(((wide_vm, w_out), (act_vm, act_out), (f_vm, f_out)))
    ]
    for copy in ins:
        copy.start()
    ins[0].wait()
    wide_vm[...] = w_vm[...].astype(jnp.float32)
    outs[0].start()
    for i in (1, 2):
        ins[i].wait()
        outs[i].start()
    for copy in outs:
        copy.wait()


def on_device(features, weight, tile_values, tile_list, train_mask, cotangent, n_blk):
    rows, feat = features.shape
    chunks = CHUNKS
    fc = feat // chunks
    sl = feat // n_blk
    bf = jnp.bfloat16
    vm = pltpu.VMEM
    dma = pltpu.SemaphoreType.DMA
    any_spec = pl.BlockSpec(memory_space=pl.ANY)
    vmem_spec = pl.BlockSpec(memory_space=pltpu.VMEM)
    act, wgrad, fgrad = pl.pallas_call(
        functools.partial(kernel, n_blk, chunks, X_CHUNKS, G_CHUNKS, W_CHUNKS),
        out_shape=(
            jax.ShapeDtypeStruct((rows, feat), bf),
            jax.ShapeDtypeStruct((n_blk, sl, feat), bf),
            jax.ShapeDtypeStruct((rows, feat), bf),
        ),
        in_specs=[
            pl.BlockSpec(memory_space=pltpu.SMEM), vmem_spec,
            any_spec, any_spec, any_spec, any_spec,
        ],
        out_specs=(vmem_spec, vmem_spec, vmem_spec),
        scratch_shapes=[
            vm((n_blk, rows, feat), bf),
            vm((n_blk, rows, feat), bf),
            vm((n_blk, sl, feat), bf),
            vm((feat, feat), bf),
            vm((n_blk, 2 * rows, rows), bf),
            vm((rows, feat), bf),
            vm((2 * rows + sl, n_blk * rows), bf),
            vm((chunks, 2, rows, fc), jnp.float32),
            vm((chunks, rows, fc), bf),
            vm((chunks, rows, fc), bf),
            vm((chunks, rows, fc), bf),
            vm((chunks, rows, fc), bf),
            vm((n_blk, sl, rows), bf),
            vm((n_blk, sl, rows), bf),
            vm((sl, feat), bf),
            vm((sl, feat), bf),
            vm((rows, feat), bf),
            vm((8, 128), bf),
            dma((4,)),
            dma((chunks, n_blk, 4)), dma((chunks, n_blk)),
            dma((chunks, n_blk, 4)), dma((chunks, n_blk)),
            dma((chunks, n_blk, 2)), dma((chunks, n_blk)),
            dma((chunks, n_blk // 4)),
            dma((n_blk,)), dma((n_blk,)),
            dma((3 * chunks,)), dma((3 * chunks,)),
        ],
        compiler_params=pltpu.CompilerParams(
            collective_id=0, has_side_effects=True, vmem_limit_bytes=56 * 1024 * 1024
        ),
    )(
        jnp.transpose(tile_list[0, 0]), train_mask.reshape(1, rows), features, weight,
        tile_values.reshape(n_blk, 2 * rows, rows), cotangent,
    )
    if not FIN:
        return act, wgrad.reshape(feat, feat).astype(jnp.float32), fgrad
    return pl.pallas_call(
        widen,
        out_shape=(
            jax.ShapeDtypeStruct((rows, feat), bf),
            jax.ShapeDtypeStruct((feat, feat), jnp.float32),
            jax.ShapeDtypeStruct((rows, feat), bf),
        ),
        in_specs=[any_spec] * 3,
        out_specs=(any_spec,) * 3,
        scratch_shapes=[
            vm((rows, feat), bf), vm((feat, feat), bf), vm((rows, feat), bf),
            vm((feat, feat), jnp.float32), dma((3,)), dma((3,)),
        ],
    )(act, wgrad.reshape(feat, feat), fgrad)


def solution(mesh):
    in_specs = (
        P(("rep", "blk"), None),
        P(),
        P("rep", "blk", None, None, None, None),
        P("rep", "blk", None, None),
        P(("rep", "blk")),
        P(("rep", "blk"), None),
    )
    out_specs = (P(("rep", "blk"), None), P(), P(("rep", "blk"), None))
    body = functools.partial(on_device, n_blk=mesh.shape["blk"])
    return jax.shard_map(
        body, mesh=mesh, in_specs=in_specs, out_specs=out_specs, check_vma=False
    )
```

```python
import functools
import math

import jax
import jax.numpy as jnp
from jax import lax
from jax.experimental import pallas as pl
from jax.experimental.pallas import tpu as pltpu
from jax.sharding import PartitionSpec as P

GELU_SCALE = math.sqrt(2.0 / math.pi)
CHUNKS = 2
X_CHUNKS = 2
G_CHUNKS = 2
W_CHUNKS = 1
T_EARLY = 0
NEAR = 1
FIN = 1
MESH = pl.DeviceIdType.MESH


def activation(pre_act):
    inner = GELU_SCALE * (pre_act + 0.044715 * pre_act * pre_act * pre_act)
    tanh_part = jnp.tanh(inner)
    act_value = 0.5 * pre_act * (1.0 + tanh_part)
    act_slope = 0.5 * (1.0 + tanh_part) + 0.5 * pre_act * (
        1.0 - tanh_part * tanh_part
    ) * GELU_SCALE * (1.0 + 3.0 * 0.044715 * pre_act * pre_act)
    return (act_value, act_slope)


def kernel(
    n_blk, chunks, xc, gc, wc,
    list_ref, mask_ref, x_ref, w_ref, tiles_ref, cot_ref,
    act_ref, wgrad_ref, fgrad_ref,
    xg, gg, wg, w_vm, tiles_vm, cot_vm, a2d, part, axs, axr, qs, qr,
    t_send, t_recv, wxs, wxr, ax_b, act_vm, fgrad_vm,
    local_sem, x_send, x_recv, g_send, g_recv, w_send, w_recv, wz_send,
    t_ssem, t_rsem, e_send, e_recv,
):
    nz = n_blk // 4
    rows = x_ref.shape[0]
    feat = x_ref.shape[1]
    fc = feat // chunks
    sl = feat // n_blk
    r = lax.axis_index("rep")
    me = lax.axis_index("blk")
    z = me // 4
    y = (me // 2) % 2
    core = me % 2

    def at(zz, yy, cc):
        return zz * 4 + yy * 2 + cc

    y_dev = at(z, 1 - y, core)
    p_dev = at(z, y, 1 - core)

    loads = [
        pltpu.make_async_copy(x_ref, xg.at[me], local_sem.at[3])
    ]
    others = [
        pltpu.make_async_copy(tiles_ref, tiles_vm, local_sem.at[0]),
        pltpu.make_async_copy(w_ref, w_vm, local_sem.at[1]),
        pltpu.make_async_copy(cot_ref, cot_vm, local_sem.at[2]),
    ]
    for copy in loads + others:
        copy.start()

    barrier = pltpu.get_barrier_semaphore()
    if NEAR:
        near = [(None, y_dev), (None, p_dev), (z > 0, at(z - 1, y, core)),
                (z < nz - 1, at(z + 1, y, core))]
    else:
        near = [(None, (me + k) % n_blk) for k in range(1, n_blk)]
    for cond, dev in near:
        def greet(dev=dev):
            pl.semaphore_signal(barrier, inc=1, device_id=(r, dev), device_id_type=MESH)
        if cond is None:
            greet()
        else:
            pl.when(cond)(greet)
    pl.semaphore_signal(barrier, inc=1, device_id=(1 - r, me), device_id_type=MESH)
    for copy in loads:
        copy.wait()
    if NEAR:
        ends = (z == 0).astype(jnp.int32) + (z == nz - 1).astype(jnp.int32)
        pl.semaphore_wait(barrier, 5 - ends)
    else:
        pl.semaphore_wait(barrier, n_blk)

    pending = []

    def send(cond, make):
        if cond is None:
            make().start()
        else:
            @pl.when(cond)
            def _():
                make().start()
        pending.append((cond, make))

    def block_copy(buf, ssem, rsem, slot, c, way, dev):
        def make():
            return pltpu.make_async_remote_copy(
                src_ref=buf(c, slot), dst_ref=buf(c, slot),
                send_sem=ssem.at[c, slot, way], recv_sem=rsem.at[c, slot],
                device_id=(r, dev), device_id_type=MESH,
            )
        return make

    def wait_block(buf, ssem, rsem, slot, c):
        pltpu.make_async_remote_copy(
            src_ref=buf(c, slot), dst_ref=buf(c, slot),
            send_sem=ssem.at[c, slot, 0], recv_sem=rsem.at[c, slot],
            device_id=(r, y_dev), device_id_type=MESH,
        ).wait_recv()

    def gather_own(buf, ssem, rsem, c):
        send(z < nz - 1, block_copy(buf, ssem, rsem, me, c, 0, at(z + 1, y, core)))
        send(z > 0, block_copy(buf, ssem, rsem, me, c, 1, at(z - 1, y, core)))
        send(None, block_copy(buf, ssem, rsem, me, c, 2, y_dev))
        send(None, block_copy(buf, ssem, rsem, me, c, 3, p_dev))

    def from_y(buf, ssem, rsem, zz, c, cond):
        slot = at(zz, 1 - y, core)
        go = block_copy(buf, ssem, rsem, slot, c, 3, p_dev)
        if cond is None:
            wait_block(buf, ssem, rsem, slot, c)
            go().start()
        else:
            @pl.when(cond)
            def _():
                wait_block(buf, ssem, rsem, slot, c)
                go().start()
        pending.append((cond, go))

    def from_z(buf, ssem, rsem, d, c, up):
        zz = z - d if up else z + d
        cond = (zz >= 0) if up else (zz < nz)
        slot = at(zz, y, core)
        nxt = z + 1 if up else z - 1
        more = (nxt < nz) if up else (nxt >= 0)
        go_z = block_copy(buf, ssem, rsem, slot, c, 0 if up else 1, at(nxt, y, core))
        go_y = block_copy(buf, ssem, rsem, slot, c, 2, y_dev)
        go_p = block_copy(buf, ssem, rsem, slot, c, 3, p_dev)

        @pl.when(cond)
        def _():
            wait_block(buf, ssem, rsem, slot, c)

            @pl.when(more)
            def _():
                go_z().start()

            go_y().start()
            go_p().start()

        pending.append((jnp.logical_and(cond, more), go_z))
        pending.append((cond, go_y))
        pending.append((cond, go_p))

    def gather_rest(buf, ssem, rsem, chunks):
        for d in range(1, nz):
            for c in range(chunks):
                from_z(buf, ssem, rsem, d, c, True)
                from_z(buf, ssem, rsem, d, c, False)
                if d == 1:
                    from_y(buf, ssem, rsem, z, c, None)
                else:
                    from_y(buf, ssem, rsem, z - d + 1, c, z - d + 1 >= 0)
                    from_y(buf, ssem, rsem, z + d - 1, c, z + d - 1 < nz)

    def gather_last(buf, ssem, rsem, c):
        d = nz
        if d == 1:
            from_y(buf, ssem, rsem, z, c, None)
        else:
            from_y(buf, ssem, rsem, z - d + 1, c, z - d + 1 >= 0)
            from_y(buf, ssem, rsem, z + d - 1, c, z + d - 1 < nz)
        for yy in range(2):
            for zz in range(nz):
                wait_block(buf, ssem, rsem, at(zz, yy, 1 - core), c)

    def exchange(src, dst, k):
        def make():
            return pltpu.make_async_remote_copy(
                src_ref=src, dst_ref=dst, send_sem=e_send.at[k], recv_sem=e_recv.at[k],
                device_id=(1 - r, me), device_id_type=MESH,
            )
        return make

    def xbuf(c, slot):
        return xg.at[slot, :, pl.ds(c * (feat // xc), feat // xc)]

    def gbuf(c, slot):
        return gg.at[slot, :, pl.ds(c * (feat // gc), feat // gc)]

    def wbuf(c, slot):
        return wg.at[slot, :, pl.ds(c * (feat // wc), feat // wc)]

    for c in range(xc):
        gather_own(xbuf, x_send, x_recv, c)

    others[0].wait()
    for j in range(n_blk):
        for h in range(2):
            here = jnp.logical_or(list_ref[0, j] == h, list_ref[1, j] == h)
            keep = jnp.where(here, 1.0, 0.0).astype(jnp.float32)
            tile = tiles_vm[j, h * rows:(h + 1) * rows, :].astype(jnp.float32) * keep
            a2d[h * rows:(h + 1) * rows, j * rows:(j + 1) * rows] = tile.astype(jnp.bfloat16)

    others[1].wait()
    others[2].wait()
    mask_cols = jnp.transpose(
        jnp.broadcast_to(mask_ref[...].astype(jnp.float32), (rows, rows))
    )
    gather_rest(xbuf, x_send, x_recv, xc)
    ax_sends = []
    for c in range(chunks):
        if c < xc:
            gather_last(xbuf, x_send, x_recv, c)
        total = jnp.dot(
            a2d[:2 * rows, :], xg[:, :, c * fc:(c + 1) * fc].reshape(n_blk * rows, fc),
            preferred_element_type=jnp.float32,
        )
        part[c] = total.reshape(2, rows, fc)
        axs[c] = part[c, 1 - r].astype(jnp.bfloat16)
        make = exchange(axs.at[c], axr.at[c], c)
        send(None, make)
        ax_sends.append(make)

    for c in range(chunks):
        ax_sends[c]().wait_recv()
        ax = part[c, r] + axr[c].astype(jnp.float32)
        ax_b[:, c * fc:(c + 1) * fc] = ax.astype(jnp.bfloat16)

    def send_slices():
        for c in range(chunks):
            ax = ax_b[:, c * fc:(c + 1) * fc].astype(jnp.float32)
            slices = jnp.transpose(ax).reshape(fc // sl, sl, rows)
            t_send[c * (fc // sl):(c + 1) * (fc // sl)] = slices.astype(jnp.bfloat16)
        t_copies = []
        for k in range(1, n_blk):
            peer = (me + k) % n_blk
            def t_make(peer=peer, k=k):
                return pltpu.make_async_remote_copy(
                    src_ref=t_send.at[peer], dst_ref=t_recv.at[me],
                    send_sem=t_ssem.at[k], recv_sem=t_rsem.at[k],
                    device_id=(r, peer), device_id_type=MESH,
                )
            send(None, t_make)
            t_copies.append(t_make)
        t_recv[me] = t_send[me]

    if T_EARLY:
        send_slices()

    for c in range(chunks):
        summed = jnp.dot(
            ax_b[...], w_vm[:, c * fc:(c + 1) * fc], preferred_element_type=jnp.float32
        )
        act_value, act_slope = activation(summed)
        act_vm[:, c * fc:(c + 1) * fc] = act_value.astype(jnp.bfloat16)
        keep = jnp.concatenate([mask_cols] * (fc // rows), axis=1)
        cot = cot_vm[:, c * fc:(c + 1) * fc].astype(jnp.float32)
        gg[me, :, c * fc:(c + 1) * fc] = (cot * keep * act_slope).astype(jnp.bfloat16)
        if gc == chunks:
            gather_own(gbuf, g_send, g_recv, c)
    if gc == 1:
        gather_own(gbuf, g_send, g_recv, 0)

    if not T_EARLY:
        send_slices()
    act_out = pltpu.make_async_copy(act_vm, act_ref, local_sem.at[0])
    act_out.start()

    gather_rest(gbuf, g_send, g_recv, gc)
    for k in range(1, n_blk):
        origin = (me + n_blk - k) % n_blk
        pltpu.make_async_remote_copy(
            src_ref=t_send.at[origin], dst_ref=t_recv.at[origin],
            send_sem=t_ssem.at[k], recv_sem=t_rsem.at[k],
            device_id=(r, origin), device_id_type=MESH,
        ).wait_recv()
    for j in range(n_blk):
        a2d[2 * rows:2 * rows + sl, j * rows:(j + 1) * rows] = t_recv[j]

    q_makes, w_makes = [], []
    for c in range(chunks):
        if c < gc:
            gather_last(gbuf, g_send, g_recv, c)
        total = jnp.dot(
            a2d[...], gg[:, :, c * fc:(c + 1) * fc].reshape(n_blk * rows, fc), preferred_element_type=jnp.float32
        )
        wxs[:, c * fc:(c + 1) * fc] = total[2 * rows:, :].astype(jnp.bfloat16)
        if wc == chunks:
            cols = pl.ds(c * fc, fc)
            make = exchange(wxs.at[:, cols], wxr.at[:, cols], chunks + c)
            send(None, make)
            w_makes.append(make)
        elif c == chunks - 1:
            make = exchange(wxs, wxr, chunks)
            send(None, make)
            w_makes.append(make)
        part[c] = total[:2 * rows, :].reshape(2, rows, fc)
        qs[c] = part[c, 1 - r].astype(jnp.bfloat16)
        make = exchange(qs.at[c], qr.at[c], 2 * chunks + c)
        send(None, make)
        q_makes.append(make)

    wf = feat // wc
    for c in range(wc):
        w_makes[c]().wait_recv()
        cols = slice(c * wf, (c + 1) * wf)
        both = wxs[:, cols].astype(jnp.float32) + wxr[:, cols].astype(jnp.float32)
        wg[me, :, cols] = both.astype(jnp.bfloat16)
        for zz in range(nz):
            def z_make(zz=zz, c=c):
                return pltpu.make_async_remote_copy(
                    src_ref=wbuf(c, me), dst_ref=wbuf(c, me),
                    send_sem=wz_send.at[c, zz], recv_sem=w_recv.at[c, me],
                    device_id=(r, at(zz, y, core)), device_id_type=MESH,
                )
            send(z != zz, z_make)
        send(None, block_copy(wbuf, w_send, w_recv, me, c, 0, y_dev))
        send(None, block_copy(wbuf, w_send, w_recv, me, c, 1, p_dev))

    fgrad = jnp.zeros((rows, feat), jnp.float32)
    for c in range(chunks):
        q_makes[c]().wait_recv()
        prop = (part[c, r] + qr[c].astype(jnp.float32)).astype(jnp.bfloat16)
        fgrad = fgrad + lax.dot_general(
            prop, w_vm[:, c * fc:(c + 1) * fc], (((1,), (1,)), ((), ())),
            preferred_element_type=jnp.float32,
        )
    fgrad_vm[...] = fgrad.astype(jnp.bfloat16)
    fgrad_out = pltpu.make_async_copy(fgrad_vm, fgrad_ref, local_sem.at[1])
    fgrad_out.start()

    for c in range(wc):
        for d in range(1, nz):
            for up in (True, False):
                zz = z - d if up else z + d
                cond = (zz >= 0) if up else (zz < nz)
                slot = at(zz, y, core)
                go_y = block_copy(wbuf, w_send, w_recv, slot, c, 0, y_dev)
                go_p = block_copy(wbuf, w_send, w_recv, slot, c, 1, p_dev)

                @pl.when(cond)
                def _():
                    wait_block(wbuf, w_send, w_recv, slot, c)
                    go_y().start()
                    go_p().start()

                pending.append((cond, go_y))
                pending.append((cond, go_p))
        for zz in range(nz):
            slot = at(zz, 1 - y, core)
            go_p = block_copy(wbuf, w_send, w_recv, slot, c, 1, p_dev)
            wait_block(wbuf, w_send, w_recv, slot, c)
            go_p().start()
            pending.append((None, go_p))
    for c in range(wc):
        for yy in range(2):
            for zz in range(nz):
                wait_block(wbuf, w_send, w_recv, at(zz, yy, 1 - core), c)
    w_out = pltpu.make_async_copy(wg, wgrad_ref, local_sem.at[2])
    w_out.start()

    for cond, make in pending:
        if cond is None:
            make().wait_send()
        else:
            @pl.when(cond)
            def _():
                make().wait_send()

    act_out.wait()
    fgrad_out.wait()
    w_out.wait()


def widen(act_in, w_in, f_in, act_out, w_out, f_out, act_vm, w_vm, f_vm, wide_vm, in_sem, out_sem):
    ins = [
        pltpu.make_async_copy(src, dst, in_sem.at[i])
        for i, (src, dst) in enumerate(((w_in, w_vm), (act_in, act_vm), (f_in, f_vm)))
    ]
    outs = [
        pltpu.make_async_copy(src, dst, out_sem.at[i])
        for i, (src, dst) in enumerate(((wide_vm, w_out), (act_vm, act_out), (f_vm, f_out)))
    ]
    for copy in ins:
        copy.start()
    ins[0].wait()
    wide_vm[...] = w_vm[...].astype(jnp.float32)
    outs[0].start()
    for i in (1, 2):
        ins[i].wait()
        outs[i].start()
    for copy in outs:
        copy.wait()


def on_device(features, weight, tile_values, tile_list, train_mask, cotangent, n_blk):
    rows, feat = features.shape
    chunks = CHUNKS
    fc = feat // chunks
    sl = feat // n_blk
    bf = jnp.bfloat16
    vm = pltpu.VMEM
    dma = pltpu.SemaphoreType.DMA
    any_spec = pl.BlockSpec(memory_space=pl.ANY)
    vmem_spec = pl.BlockSpec(memory_space=pltpu.VMEM)
    act, wgrad, fgrad = pl.pallas_call(
        functools.partial(kernel, n_blk, chunks, X_CHUNKS, G_CHUNKS, W_CHUNKS),
        out_shape=(
            jax.ShapeDtypeStruct((rows, feat), bf),
            jax.ShapeDtypeStruct((n_blk, sl, feat), bf),
            jax.ShapeDtypeStruct((rows, feat), bf),
        ),
        in_specs=[
            pl.BlockSpec(memory_space=pltpu.SMEM), vmem_spec,
            any_spec, any_spec, any_spec, any_spec,
        ],
        out_specs=(any_spec, any_spec, any_spec),
        scratch_shapes=[
            vm((n_blk, rows, feat), bf),
            vm((n_blk, rows, feat), bf),
            vm((n_blk, sl, feat), bf),
            vm((feat, feat), bf),
            vm((n_blk, 2 * rows, rows), bf),
            vm((rows, feat), bf),
            vm((2 * rows + sl, n_blk * rows), bf),
            vm((chunks, 2, rows, fc), jnp.float32),
            vm((chunks, rows, fc), bf),
            vm((chunks, rows, fc), bf),
            vm((chunks, rows, fc), bf),
            vm((chunks, rows, fc), bf),
            vm((n_blk, sl, rows), bf),
            vm((n_blk, sl, rows), bf),
            vm((sl, feat), bf),
            vm((sl, feat), bf),
            vm((rows, feat), bf),
            vm((rows, feat), bf),
            vm((rows, feat), bf),
            dma((4,)),
            dma((chunks, n_blk, 4)), dma((chunks, n_blk)),
            dma((chunks, n_blk, 4)), dma((chunks, n_blk)),
            dma((chunks, n_blk, 2)), dma((chunks, n_blk)),
            dma((chunks, n_blk // 4)),
            dma((n_blk,)), dma((n_blk,)),
            dma((3 * chunks,)), dma((3 * chunks,)),
        ],
        compiler_params=pltpu.CompilerParams(
            collective_id=0, has_side_effects=True, vmem_limit_bytes=56 * 1024 * 1024
        ),
    )(
        jnp.transpose(tile_list[0, 0]), train_mask.reshape(1, rows), features, weight,
        tile_values.reshape(n_blk, 2 * rows, rows), cotangent,
    )
    if not FIN:
        return act, wgrad.reshape(feat, feat).astype(jnp.float32), fgrad
    return pl.pallas_call(
        widen,
        out_shape=(
            jax.ShapeDtypeStruct((rows, feat), bf),
            jax.ShapeDtypeStruct((feat, feat), jnp.float32),
            jax.ShapeDtypeStruct((rows, feat), bf),
        ),
        in_specs=[any_spec] * 3,
        out_specs=(any_spec,) * 3,
        scratch_shapes=[
            vm((rows, feat), bf), vm((feat, feat), bf), vm((rows, feat), bf),
            vm((feat, feat), jnp.float32), dma((3,)), dma((3,)),
        ],
    )(act, wgrad.reshape(feat, feat), fgrad)


def solution(mesh):
    in_specs = (
        P(("rep", "blk"), None),
        P(),
        P("rep", "blk", None, None, None, None),
        P("rep", "blk", None, None),
        P(("rep", "blk")),
        P(("rep", "blk"), None),
    )
    out_specs = (P(("rep", "blk"), None), P(), P(("rep", "blk"), None))
    body = functools.partial(on_device, n_blk=mesh.shape["blk"])
    return jax.shard_map(
        body, mesh=mesh, in_specs=in_specs, out_specs=out_specs, check_vma=False
    )
```
